128 devices in a mesh: scan: 32 (over z, x, core), col: 4 (over y).
Axes of the slice: x: 4, y: 4, z: 4, core: 2. Of those that a mesh axis runs over, the one named last changes fastest.
Arguments:
- object_field: float32 [2, 8192, 1024], P(None, 'scan', 'col'), may hold values from -6 to 6
- amplitudes: bfloat16 [256, 256, 256], P(('scan', 'col')), may hold values from 0.099609375 to 3
- positions: int32 [256, 2], P(('scan', 'col')), may hold values from 0 to 7936, as said below
- frame_count: int32 [128], P(('scan', 'col')), may hold values from 1 to 2, as said below
- coefficients: float32 [256, 4], P(('scan', 'col')), may hold values from -6 to 6
- probe_modes: float32 [4, 2, 256, 256], replicated, may hold values from -6 to 6
Outputs:
- refined_object: float32 [2, 8192, 1024], P(None, 'scan', 'col')
- refined_modes: float32 [4, 2, 256, 256], replicated
- refined_coefficients: float32 [256, 4], P(('scan', 'col'))
The draws below stay inside these ranges and needn't reach their ends.
Inputs may be any that keep to these rules, and one draw needn't show every extreme that they name: `positions`: frame g belongs to the device of index g // 2 along scan+col (scan slowest). Its top-left pixel lies in that device's block of 256 x 256 pixels, and its 256 x 256 patch lies inside the object. Entry d counts the live frames of the device of index d along scan+col: its first frame_count[d] slots are live, the rest are ignored. Some device has 2.
All inputs are finite; a program needn't handle non-finite values.
Results may differ from the reference program's by a relative error of at most 0.0058.
Values sent between devices are 32-bit elements; how exact they have to be, the bound alone decides.
No kernel may reach another device: no remote copies, remote signals or barrier semaphores. Data moves between devices by JAX's collectives and lax.ppermute only.
A program may use at most 128 MiB of HBM per device.

```python
import math
import jax
import jax.numpy as jnp
from jax import lax

FS = 256
MODES = 4
ITERS = 2
F_DEV = 2
BH = 256
BW = 256
FRAMES = 256
OH = 8192
OW = 1024
N_SCAN = 32
N_COL = 4


def draw_positions(key, part):
    devices = N_SCAN * N_COL
    frames = F_DEV * devices
    slot_index = jnp.arange(frames, dtype=jnp.int32)
    device = slot_index // F_DEV
    scan_index = device // N_COL
    col_index = device % N_COL
    row_key, col_key = jax.random.split(jax.random.fold_in(key, 11))
    row_limit = jnp.where(scan_index < N_SCAN - 1, BH, BH - FS + 1).astype(jnp.int32)
    col_limit = jnp.where(col_index < N_COL - 1, BW, BW - FS + 1).astype(jnp.int32)
    row_offset = jax.random.randint(row_key, (frames,), 0, row_limit, dtype=jnp.int32)
    col_offset = jax.random.randint(col_key, (frames,), 0, col_limit, dtype=jnp.int32)
    return jnp.stack([scan_index * BH + row_offset, col_index * BW + col_offset], 1).astype(jnp.int32)


def draw_frame_count(key, part):
    devices = N_SCAN * N_COL
    pick_key, count_key = jax.random.split(jax.random.fold_in(key, 23))
    raw_draw = jax.random.randint(count_key, (devices,), 0, F_DEV, dtype=jnp.int32)
    counts = jnp.maximum(1, raw_draw * raw_draw // F_DEV)
    chosen = jax.random.randint(pick_key, (), 0, devices, dtype=jnp.int32)
    return jnp.where(jnp.arange(devices, dtype=jnp.int32) == chosen, F_DEV, counts).astype(jnp.int32)


def block_scale(stream_key, extent, shards, least, top_value):
    gain = 1.0
    for position, shards_of in shards:
        draws = jax.random.uniform(jax.random.fold_in(jax.random.fold_in(stream_key, 6), position), (shards_of,), jnp.float32, least / len(shards), top_value / len(shards))
        gain = gain * jnp.repeat(jnp.exp(draws), extent[position] // shards_of).reshape((-1,) + (1,) * (len(extent) - 1 - position))
    return gain


def scatter_about(stream_key, shape, deviation, most, pieces=(), kind=jnp.bfloat16):
    drawn = jax.random.normal(stream_key, shape, jnp.float32) * deviation
    if len(pieces) > 0:
        drawn = block_scale(stream_key, shape, pieces, -0.22, 0.18) * drawn
    return jnp.clip(drawn, min=-most, max=most).astype(kind)


def setup_inputs(seed: int = 0) -> dict:
    splits = jax.random.split(jax.random.key(seed), 7)
    object_field = scatter_about(splits[0], (2, OH, OW), 1.0, 6.0, ((1, 32), (2, 4)), jnp.float32)
    amplitudes = jnp.clip(jnp.exp(math.log(3.0) - 3.4051113 * jax.random.uniform(splits[1], (FRAMES, FS, FS), jnp.float32) ** block_scale(splits[1], (FRAMES, FS, FS), ((0, 128),), -0.2, 0.2)), 0.099609375, 3.0).astype(jnp.bfloat16)
    positions = draw_positions(jax.random.fold_in(splits[6], 71), 0)
    frame_count = draw_frame_count(jax.random.fold_in(splits[6], 71), 0)
    coefficients = scatter_about(splits[4], (FRAMES, MODES), 1.0, 6.0, ((0, 128),), jnp.float32)
    probe_modes = scatter_about(splits[5], (MODES, 2, FS, FS), 1.0, 6.0, (), jnp.float32)
    return dict(object_field=object_field, amplitudes=amplitudes, positions=positions, frame_count=frame_count, coefficients=coefficients, probe_modes=probe_modes)


highest = lax.Precision.HIGHEST

def make_tables(length):
    indices = jnp.arange(length, dtype=jnp.int32)
    phases = indices[:, None] * indices[None, :] % length
    angles = phases.astype(jnp.float32) * (2.0 * math.pi / length)
    factor = 1.0 / math.sqrt(length)
    cosine = jnp.cos(angles) * factor
    sine_table = jnp.sin(angles) * factor
    rows_table = jnp.concatenate([jnp.concatenate([cosine, sine_table], 1), jnp.concatenate([-sine_table, cosine], 1)], 0)
    cols_table = jnp.concatenate([jnp.concatenate([cosine, -sine_table], 1), jnp.concatenate([sine_table, cosine], 1)], 0)
    return (rows_table.astype(jnp.bfloat16), cols_table.astype(jnp.bfloat16))

def apply_transform(real_part, imag_part, first_table, second_table):
    length = real_part.shape[0]
    stacked = jnp.concatenate([real_part, imag_part], 0)
    halfway = jnp.dot(first_table, stacked, preferred_element_type=jnp.float32).astype(jnp.bfloat16)
    beside = jnp.concatenate([halfway[:length], halfway[length:]], 1)
    result = jnp.dot(beside, second_table, preferred_element_type=jnp.float32)
    return (result[:, :length], result[:, length:])

def frame_update(object_patch, probe_field, amplitude, rows_table, cols_table):
    probe_real = probe_field[0]
    probe_imag = probe_field[1]
    object_real = object_patch[0]
    object_imag = object_patch[1]
    exit_real = probe_real * object_real - probe_imag * object_imag
    exit_imag = probe_real * object_imag + probe_imag * object_real
    far_real, far_imag = apply_transform(exit_real.astype(jnp.bfloat16), exit_imag.astype(jnp.bfloat16), rows_table, cols_table)
    magnitude = jnp.sqrt(far_real * far_real + far_imag * far_imag)
    factor = amplitude.astype(jnp.float32) / jnp.maximum(magnitude, 0.5)
    new_real, new_imag = apply_transform((far_real * factor).astype(jnp.bfloat16), (far_imag * factor).astype(jnp.bfloat16), cols_table, rows_table)
    diff_real = new_real - exit_real
    diff_imag = new_imag - exit_imag
    update = jnp.stack([probe_real * diff_real + probe_imag * diff_imag, probe_real * diff_imag - probe_imag * diff_real, probe_real * probe_real + probe_imag * probe_imag])
    probe_step = jnp.stack([object_real * diff_real + object_imag * diff_imag, object_real * diff_imag - object_imag * diff_real])
    return (update, probe_step)

def gram_parts(flat_modes):
    real_plane = flat_modes[:, 0]
    imag_plane = flat_modes[:, 1]
    gram_real = jnp.dot(real_plane, real_plane.T, precision=highest, preferred_element_type=jnp.float32) + jnp.dot(imag_plane, imag_plane.T, precision=highest, preferred_element_type=jnp.float32)
    gram_imag = jnp.dot(real_plane, imag_plane.T, precision=highest, preferred_element_type=jnp.float32) - jnp.dot(imag_plane, real_plane.T, precision=highest, preferred_element_type=jnp.float32)
    return (gram_real, gram_imag)

def orthonormal(flat_modes, gram_real, gram_imag):
    mode_count = flat_modes.shape[0]
    upper_real = [[None] * mode_count for other in range(mode_count)]
    upper_imag = [[None] * mode_count for other in range(mode_count)]
    for right_index in range(mode_count):
        for left_index in range(right_index):
            sum_real = gram_real[left_index, right_index]
            sum_imag = gram_imag[left_index, right_index]
            for inner_index in range(left_index):
                first_real = upper_real[inner_index][left_index]
                first_imag = upper_imag[inner_index][left_index]
                second_real = upper_real[inner_index][right_index]
                second_imag = upper_imag[inner_index][right_index]
                sum_real = sum_real - (first_real * second_real + first_imag * second_imag)
                sum_imag = sum_imag - (first_real * second_imag - first_imag * second_real)
            upper_real[left_index][right_index] = sum_real / upper_real[left_index][left_index]
            upper_imag[left_index][right_index] = sum_imag / upper_real[left_index][left_index]
        diagonal = gram_real[right_index, right_index]
        for inner_index in range(right_index):
            entry_real = upper_real[inner_index][right_index]
            entry_imag = upper_imag[inner_index][right_index]
            diagonal = diagonal - (entry_real * entry_real + entry_imag * entry_imag)
        upper_real[right_index][right_index] = jnp.sqrt(diagonal)
    columns = []
    for right_index in range(mode_count):
        vector_real = flat_modes[right_index, 0]
        vector_imag = flat_modes[right_index, 1]
        for left_index in range(right_index):
            basis_real, basis_imag = columns[left_index]
            entry_real = upper_real[left_index][right_index]
            entry_imag = upper_imag[left_index][right_index]
            vector_real = vector_real - (entry_real * basis_real - entry_imag * basis_imag)
            vector_imag = vector_imag - (entry_real * basis_imag + entry_imag * basis_real)
        pivot = upper_real[right_index][right_index]
        columns.append((vector_real / pivot, vector_imag / pivot))
    return jnp.stack([jnp.stack([pair[0], pair[1]]) for pair in columns])

def reference(object_field, amplitudes, positions, frame_count, coefficients, probe_modes):
    frames = amplitudes.shape[0]
    length = amplitudes.shape[1]
    mode_count = probe_modes.shape[0]
    pixels = length * length
    root_total = math.sqrt(frames)
    rows_table, cols_table = make_tables(length)
    slot_index = jnp.arange(frames, dtype=jnp.int32)
    owner = (slot_index // F_DEV).astype(jnp.int32)
    live_mask = slot_index % F_DEV < frame_count[owner]
    anchor = jnp.zeros((), jnp.int32)
    for iteration in range(ITERS):
        current_object = object_field
        current_modes = probe_modes

        def visit(state, item):
            amplitude, offset, weights, alive = item

            def work(inner):
                totals, mode_terms = inner
                object_patch = lax.dynamic_slice(current_object, (anchor, offset[0], offset[1]), (2, length, length))
                probe_field = jnp.tensordot(weights, current_modes, axes=1, precision=highest)
                update, probe_step = frame_update(object_patch, probe_field, amplitude, rows_table, cols_table)
                window = lax.dynamic_slice(totals, (anchor, offset[0], offset[1]), (3, length, length))
                totals = lax.dynamic_update_slice(totals, window + update, (anchor, offset[0], offset[1]))
                mode_terms = mode_terms + weights[:, None, None, None] * probe_step[None]
                return ((totals, mode_terms), probe_step)

            def skip(inner):
                return (inner, jnp.zeros((2, length, length), jnp.float32))
            return lax.cond(alive, work, skip, state)
        initial = (jnp.zeros((3,) + object_field.shape[1:], jnp.float32), jnp.zeros((mode_count, 2, length, length), jnp.float32))
        (totals, mode_terms), stashed = lax.scan(visit, initial, (amplitudes, positions, coefficients, live_mask))
        object_field = object_field + totals[:2] / (totals[2] + 1.0)
        raised = (probe_modes + mode_terms / root_total).reshape(mode_count, 2, pixels)
        gram_real, gram_imag = gram_parts(raised)
        orthogonal = orthonormal(raised, gram_real / pixels, gram_imag / pixels)
        ortho_flat = orthogonal.reshape(mode_count, 2 * pixels)
        mixing = jnp.dot(probe_modes.reshape(mode_count, 2 * pixels), ortho_flat.T, precision=highest, preferred_element_type=jnp.float32) / pixels
        projected = jnp.dot(stashed.reshape(frames, 2 * pixels), ortho_flat.T, precision=highest, preferred_element_type=jnp.float32) / pixels
        refit = jnp.dot(coefficients, mixing, precision=highest, preferred_element_type=jnp.float32) + 0.5 * projected
        coefficients = jnp.where(live_mask[:, None], refit, coefficients)
        probe_modes = orthogonal.reshape(mode_count, 2, length, length)
    return (object_field, probe_modes, coefficients)
```

```python
import functools
import math

import jax
import jax.numpy as jnp
import numpy as np
from jax import lax
from jax.experimental import pallas as pl
from jax.experimental.pallas import tpu as pltpu
from jax.sharding import Mesh
from jax.sharding import PartitionSpec as P

ITERS = 2
F32 = jnp.float32
BF16 = jnp.bfloat16
CHIPS = ("z", "x", "y")
SCAN = ("z", "x", "core")
ALL = ("z", "x", "core", "y")
ROWS = 32


def make_tables(length):
    indices = jnp.arange(length, dtype=jnp.int32)
    phases = indices[:, None] * indices[None, :] % length
    angles = phases.astype(F32) * (2.0 * math.pi / length)
    factor = 1.0 / math.sqrt(length)
    cosine = (jnp.cos(angles) * factor).astype(BF16)
    sine = (jnp.sin(angles) * factor).astype(BF16)
    return cosine, sine


def fill_tables(cos_ref, sin_ref, rows_ref, cols_ref):
    n = cos_ref.shape[0]
    cosine = cos_ref[...]
    sine = sin_ref[...]
    rows_ref[:n, :n] = cosine
    rows_ref[:n, n:] = sine
    rows_ref[n:, :n] = -sine
    rows_ref[n:, n:] = cosine
    cols_ref[:n, :n] = cosine
    cols_ref[:n, n:] = -sine
    cols_ref[n:, :n] = sine
    cols_ref[n:, n:] = cosine


def frames_kernel(
    core_ref, pos_ref, cnt_ref, coef_ref, own_ref, right_ref, below_ref, corner_ref,
    amp_ref, modes_ref, cos_ref, sin_ref,
    keep_ref, give_ref, grads_ref, t_own_ref, t_right_ref, t_below_ref, t_corner_ref,
    ext_ref, tot_ref, probe_ref, exit_ref, rows_ref, cols_ref, stack_ref, side_ref, wide_ref,
    in_sem, out_sem,
):
    frames, n = amp_ref.shape[0], amp_ref.shape[1]
    modes = modes_ref.shape[0]
    loads = []
    for i, (src, a, b) in enumerate(
        ((own_ref, 0, 0), (right_ref, 0, n), (below_ref, n, 0), (corner_ref, n, n))
    ):
        loads.append(pltpu.make_async_copy(src, ext_ref.at[:, a : a + n, b : b + n], in_sem.at[i]))
    for load in loads:
        load.start()
    fill_tables(cos_ref, sin_ref, rows_ref, cols_ref)
    tot_ref[...] = jnp.zeros_like(tot_ref)
    is_first = core_ref[0] == 0
    offsets = [(pos_ref[f, 0] & (n - 1), pos_ref[f, 1] & (n - 1)) for f in range(frames)]
    weights = [
        [jnp.where(f < cnt_ref[0], coef_ref[f, k], 0.0) for k in range(modes)] for f in range(frames)
    ]
    for load in loads:
        load.wait()

    def patch_rows(f, plane, b):
        r, c = offsets[f]
        base = pl.multiple_of((r >> 3) * 8 + b * ROWS, 8)
        rows = ext_ref[plane, pl.ds(base, ROWS + 8), :]
        rows = pltpu.roll(rows, (2 * n - c) & (2 * n - 1), 1)[:, :n]
        return pltpu.roll(rows, ROWS + 8 - (r & 7), 0)[:ROWS]

    def start(b, carry):
        at = pl.ds(pl.multiple_of(b * ROWS, ROWS), ROWS)
        at_imag = pl.ds(pl.multiple_of(n + b * ROWS, ROWS), ROWS)
        for f in range(frames):
            o_re = patch_rows(f, 0, b)
            o_im = patch_rows(f, 1, b)
            grads_ref[f, 0, at, :] = o_re
            grads_ref[f, 1, at, :] = o_im
            p_re = weights[f][0] * modes_ref[0, 0, at, :]
            p_im = weights[f][0] * modes_ref[0, 1, at, :]
            for k in range(1, modes):
                p_re = p_re + weights[f][k] * modes_ref[k, 0, at, :]
                p_im = p_im + weights[f][k] * modes_ref[k, 1, at, :]
            probe_ref[f, 0, at, :] = p_re
            probe_ref[f, 1, at, :] = p_im
            e_re = p_re * o_re - p_im * o_im
            e_im = p_re * o_im + p_im * o_re
            exit_ref[f, 0, at, :] = e_re
            exit_ref[f, 1, at, :] = e_im
            stack_ref[at, f * n : (f + 1) * n] = e_re.astype(BF16)
            stack_ref[at_imag, f * n : (f + 1) * n] = e_im.astype(BF16)
        return carry

    lax.fori_loop(0, n // ROWS, start, 0)

    def transform(first_ref, second_ref):
        for f in range(frames):
            cols = slice(f * n, (f + 1) * n)
            for h in range(2):
                half = jnp.dot(
                    first_ref[h * n : (h + 1) * n, :], stack_ref[:, cols], preferred_element_type=F32
                )
                side_ref[cols, h * n : (h + 1) * n] = half.astype(BF16)
        for f in range(frames):
            cols = slice(f * n, (f + 1) * n)
            wide_ref[cols, :] = jnp.dot(side_ref[cols, :], second_ref[...], preferred_element_type=F32)

    transform(rows_ref, cols_ref)

    def scale(b, carry):
        at = pl.ds(pl.multiple_of(b * ROWS, ROWS), ROWS)
        at_imag = pl.ds(pl.multiple_of(n + b * ROWS, ROWS), ROWS)
        for f in range(frames):
            at_f = pl.ds(pl.multiple_of(f * n + b * ROWS, ROWS), ROWS)
            far_re = wide_ref[at_f, :n]
            far_im = wide_ref[at_f, n:]
            inverse = jnp.minimum(lax.rsqrt(far_re * far_re + far_im * far_im), 2.0)
            factor = amp_ref[f, at, :].astype(F32) * inverse
            stack_ref[at, f * n : (f + 1) * n] = (far_re * factor).astype(BF16)
            stack_ref[at_imag, f * n : (f + 1) * n] = (far_im * factor).astype(BF16)
        return carry

    lax.fori_loop(0, n // ROWS, scale, 0)
    transform(cols_ref, rows_ref)

    def finish(b, carry):
        at = pl.ds(pl.multiple_of(b * ROWS, ROWS), ROWS)
        sums = [[None, None] for _ in range(modes)]
        pad = jnp.zeros((8, n), F32)
        beside = jnp.zeros((ROWS + 8, n), F32)
        for f in range(frames):
            r, c = offsets[f]
            at_f = pl.ds(pl.multiple_of(f * n + b * ROWS, ROWS), ROWS)
            d_re = wide_ref[at_f, :n] - exit_ref[f, 0, at, :]
            d_im = wide_ref[at_f, n:] - exit_ref[f, 1, at, :]
            p_re = probe_ref[f, 0, at, :]
            p_im = probe_ref[f, 1, at, :]
            updates = (
                p_re * d_re + p_im * d_im,
                p_re * d_im - p_im * d_re,
                p_re * p_re + p_im * p_im,
            )
            for q in range(3):
                placed = pltpu.roll(jnp.concatenate([updates[q], pad], 0), r & 7, 0)
                placed = pltpu.roll(jnp.concatenate([placed, beside], 1), c, 1)
                rows = pl.ds(pl.multiple_of((r >> 3) * 8 + b * ROWS, 8), ROWS + 8)
                tot_ref[q, rows, :] = tot_ref[q, rows, :] + placed
            o_re = grads_ref[f, 0, at, :]
            o_im = grads_ref[f, 1, at, :]
            g_re = o_re * d_re + o_im * d_im
            g_im = o_re * d_im - o_im * d_re
            grads_ref[f, 0, at, :] = g_re
            grads_ref[f, 1, at, :] = g_im
            for k in range(modes):
                for q, g in ((0, g_re), (1, g_im)):
                    term = weights[f][k] * g
                    sums[k][q] = term if f == 0 else sums[k][q] + term
        for k in range(modes):
            keep = jnp.where(is_first, sums[k][0], sums[k][1])
            give = jnp.where(is_first, sums[k][1], sums[k][0])
            for i in range(ROWS // 8):
                for j in range(n // 128):
                    tile = b * (ROWS // 8 * (n // 128)) + i * (n // 128) + j
                    keep_ref[tile, k] = keep[8 * i : 8 * i + 8, 128 * j : 128 * j + 128]
                    give_ref[tile, k] = give[8 * i : 8 * i + 8, 128 * j : 128 * j + 128]
        return carry

    lax.fori_loop(0, n // ROWS, finish, 0)
    stores = []
    for i, (dst, a, b) in enumerate(
        ((t_own_ref, 0, 0), (t_right_ref, 0, n), (t_below_ref, n, 0), (t_corner_ref, n, n))
    ):
        stores.append(pltpu.make_async_copy(tot_ref.at[:, a : a + n, b : b + n], dst, out_sem.at[i]))
    for store in stores:
        store.start()
    for store in stores:
        store.wait()


def run_frames(core, positions, count, coefficients, blocks, amplitudes, modes, tables):
    frames, n = amplitudes.shape[0], amplitudes.shape[1]
    k = modes.shape[0]
    tiles = n * n // 1024
    smem = pl.BlockSpec(memory_space=pltpu.SMEM)
    vmem = pl.BlockSpec(memory_space=pltpu.VMEM)
    hbm = pl.BlockSpec(memory_space=pl.ANY)
    piece = jax.ShapeDtypeStruct((tiles, k, 8, 128), F32)
    quarter = jax.ShapeDtypeStruct((3, n, n), F32)
    return pl.pallas_call(
        frames_kernel,
        out_shape=(piece, piece, jax.ShapeDtypeStruct((frames, 2, n, n), F32)) + (quarter,) * 4,
        in_specs=[smem] * 4 + [hbm] * 4 + [vmem] * 4,
        out_specs=(vmem,) * 3 + (hbm,) * 4,
        scratch_shapes=[
            pltpu.VMEM((2, 2 * n, 2 * n), F32),
            pltpu.VMEM((3, 2 * n, 2 * n), F32),
            pltpu.VMEM((frames, 2, n, n), F32),
            pltpu.VMEM((frames, 2, n, n), F32),
            pltpu.VMEM((2 * n, 2 * n), BF16),
            pltpu.VMEM((2 * n, 2 * n), BF16),
            pltpu.VMEM((2 * n, frames * n), BF16),
            pltpu.VMEM((frames * n, 2 * n), BF16),
            pltpu.VMEM((frames * n, 2 * n), F32),
            pltpu.SemaphoreType.DMA((4,)),
            pltpu.SemaphoreType.DMA((4,)),
        ],
        name="frames",
    )(core, positions, count, coefficients, *blocks, amplitudes, modes, *tables)


def spread_kernel(got_ref, out_ref):
    total = jnp.sum(got_ref[...], axis=0)
    out_ref[...] = jnp.broadcast_to(total[None], out_ref.shape)


def run_spread(got):
    vmem = pl.BlockSpec(memory_space=pltpu.VMEM)
    return pl.pallas_call(
        spread_kernel,
        out_shape=jax.ShapeDtypeStruct(got.shape, F32),
        in_specs=[vmem],
        out_specs=vmem,
        name="spread",
    )(got)


def total_of(acc):
    across = jnp.sum(jnp.sum(acc, axis=0, keepdims=True), axis=1, keepdims=True)
    return jnp.broadcast_to(across, acc.shape)


def modes_kernel(
    core_ref, cnt_ref, coef_ref, mine_ref, other_ref, old_ref, grads_ref, new_ref, out_coef_ref, raised_ref,
    *, root_total,
):
    modes, n = old_ref.shape[0], old_ref.shape[2]
    frames = grads_ref.shape[0]
    pixels = n * n
    is_first = core_ref[0] == 0
    lanes = n // 128
    pairs = [(i, j) for j in range(modes) for i in range(j)]
    zero = jnp.zeros((8, 128), F32)

    def lift(t, acc):
        acc = list(acc)
        at = pl.ds(pl.multiple_of(t * 8, 8), 8)
        for lane in range(lanes):
            col = slice(lane * 128, lane * 128 + 128)
            tile = t * lanes + lane
            re, im = [], []
            for k in range(modes):
                mine = mine_ref[tile, k]
                other = other_ref[tile, k]
                s_re = jnp.where(is_first, mine, other)
                s_im = jnp.where(is_first, other, mine)
                re.append(old_ref[k, 0, at, col] + s_re * (1.0 / root_total))
                im.append(old_ref[k, 1, at, col] + s_im * (1.0 / root_total))
                raised_ref[k, 0, at, col] = re[k]
                raised_ref[k, 1, at, col] = im[k]
            for k in range(modes):
                acc[k] = acc[k] + (re[k] * re[k] + im[k] * im[k])
            for p, (i, j) in enumerate(pairs):
                acc[modes + 2 * p] = acc[modes + 2 * p] + (re[i] * re[j] + im[i] * im[j])
                acc[modes + 2 * p + 1] = acc[modes + 2 * p + 1] + (re[i] * im[j] - im[i] * re[j])
        return tuple(acc)

    acc = lax.fori_loop(0, n // 8, lift, (zero,) * (modes + 2 * len(pairs)))
    gram = [total_of(a) * (1.0 / pixels) for a in acc]
    upper = {}
    inverse = []
    for j in range(modes):
        for i in range(j):
            p = pairs.index((i, j))
            s_re = gram[modes + 2 * p]
            s_im = gram[modes + 2 * p + 1]
            for k in range(i):
                a_re, a_im = upper[k, i]
                b_re, b_im = upper[k, j]
                s_re = s_re - (a_re * b_re + a_im * b_im)
                s_im = s_im - (a_re * b_im - a_im * b_re)
            upper[i, j] = (s_re * inverse[i], s_im * inverse[i])
        diagonal = gram[j]
        for k in range(j):
            a_re, a_im = upper[k, j]
            diagonal = diagonal - (a_re * a_re + a_im * a_im)
        inverse.append(1.0 / jnp.sqrt(diagonal))

    def solve(t, acc):
        acc = list(acc)
        at = pl.ds(pl.multiple_of(t * 8, 8), 8)
        for lane in range(lanes):
            col = slice(lane * 128, lane * 128 + 128)
            basis = []
            for j in range(modes):
                v_re = raised_ref[j, 0, at, col]
                v_im = raised_ref[j, 1, at, col]
                for i in range(j):
                    r_re, r_im = upper[i, j]
                    q_re, q_im = basis[i]
                    v_re = v_re - (r_re * q_re - r_im * q_im)
                    v_im = v_im - (r_re * q_im + r_im * q_re)
                basis.append((v_re * inverse[j], v_im * inverse[j]))
                new_ref[j, 0, at, col] = basis[j][0]
                new_ref[j, 1, at, col] = basis[j][1]
            for j in range(modes):
                o_re = old_ref[j, 0, at, col]
                o_im = old_ref[j, 1, at, col]
                for k in range(modes):
                    s = j * modes + k
                    acc[s] = acc[s] + (basis[k][0] * o_re + basis[k][1] * o_im)
            for f in range(frames):
                g_re = grads_ref[f, 0, at, col]
                g_im = grads_ref[f, 1, at, col]
                for k in range(modes):
                    s = (modes + f) * modes + k
                    acc[s] = acc[s] + (basis[k][0] * g_re + basis[k][1] * g_im)
        return tuple(acc)

    acc = lax.fori_loop(0, n // 8, solve, (zero,) * ((modes + frames) * modes))
    dots = [jnp.sum(a) * (1.0 / pixels) for a in acc]
    for f in range(frames):
        for k in range(modes):
            value = 0.5 * dots[(modes + f) * modes + k]
            for j in range(modes):
                value = value + coef_ref[f, j] * dots[j * modes + k]
            out_coef_ref[f, k] = jnp.where(f < cnt_ref[0], value, coef_ref[f, k])


def run_modes(core, count, coefficients, mine, other, old, grads, root_total):
    smem = pl.BlockSpec(memory_space=pltpu.SMEM)
    vmem = pl.BlockSpec(memory_space=pltpu.VMEM)
    return pl.pallas_call(
        functools.partial(modes_kernel, root_total=root_total),
        out_shape=(
            jax.ShapeDtypeStruct(old.shape, F32),
            jax.ShapeDtypeStruct(coefficients.shape, F32),
        ),
        in_specs=[smem] * 3 + [vmem] * 4,
        out_specs=(vmem, smem),
        scratch_shapes=[pltpu.VMEM(old.shape, F32)],
        name="modes",
    )(core, count, coefficients, mine, other, old, grads)


def moves(scans, cols, down, over):
    pairs = []
    for s in range(scans):
        for c in range(cols):
            if 0 <= s + down < scans and 0 <= c + over < cols:
                pairs.append((s * cols + c, (s + down) * cols + c + over))
    return pairs


def on_device(object_field, amplitudes, positions, frame_count, coefficients, probe_modes):
    frames, length = amplitudes.shape[0], amplitudes.shape[1]
    cols = lax.axis_size("y")
    scans = lax.axis_size(SCAN)
    root_total = math.sqrt(frames * scans * cols)
    core = lax.axis_index("core").astype(jnp.int32).reshape(1)
    swap = [(0, 1), (1, 0)]

    def widen(block):
        corner = lax.ppermute(block, ALL, moves(scans, cols, -1, -1))
        right = lax.ppermute(block, ALL, moves(scans, cols, 0, -1))
        below = lax.ppermute(block, ALL, moves(scans, cols, -1, 0))
        return [block, right, below, corner]

    tables = make_tables(length)
    blocks = widen(object_field)
    for iteration in range(ITERS):
        keep, give, grads, t_own, t_right, t_below, t_corner = run_frames(
            core, positions, frame_count, coefficients, blocks, amplitudes, probe_modes, tables
        )
        kept = keep + lax.ppermute(give, "core", swap)
        crossed = lax.ppermute(t_corner, ALL, moves(scans, cols, 1, 1))
        arrived = lax.ppermute(t_right, ALL, moves(scans, cols, 0, 1))
        lowered = lax.ppermute(t_below, ALL, moves(scans, cols, 1, 0))
        got = lax.all_to_all(kept, CHIPS, split_axis=0, concat_axis=0, tiled=True)
        settled = t_own + arrived + lowered + crossed
        object_field = object_field + settled[:2] / (settled[2] + 1.0)
        if iteration + 1 < ITERS:
            blocks = widen(object_field)
            got, object_field = lax.optimization_barrier((got, object_field))
        spread = run_spread(got)
        mine = lax.all_to_all(spread, CHIPS, split_axis=0, concat_axis=0, tiled=True)
        other = lax.ppermute(mine, "core", swap)
        probe_modes, coefficients = run_modes(
            core, frame_count, coefficients, mine, other, probe_modes, grads, root_total
        )
    return (object_field, probe_modes, coefficients)


def solution(mesh):
    scans, cols = mesh.shape["scan"], mesh.shape["col"]
    fine = Mesh(np.asarray(mesh.devices).reshape(4, scans // 8, 2, cols), ALL)
    placed = (
        P(None, SCAN, "y"),
        P(ALL, None, None),
        P(ALL, None),
        P(ALL),
        P(ALL, None),
        P(),
    )
    return jax.shard_map(
        on_device,
        mesh=fine,
        in_specs=placed,
        out_specs=(P(None, SCAN, "y"), P(), P(ALL, None)),
        check_vma=False,
    )
```

```python
import functools
import math

import jax
import jax.numpy as jnp
import numpy as np
from jax import lax
from jax.experimental import pallas as pl
from jax.experimental.pallas import tpu as pltpu
from jax.sharding import Mesh
from jax.sharding import PartitionSpec as P

ITERS = 2
F32 = jnp.float32
BF16 = jnp.bfloat16
CHIPS = ("z", "x", "y")
SCAN = ("z", "x", "core")
ALL = ("z", "x", "core", "y")
ROWS = 32


def make_tables(length):
    indices = jnp.arange(length, dtype=jnp.int32)
    phases = indices[:, None] * indices[None, :] % length
    angles = phases.astype(F32) * (2.0 * math.pi / length)
    factor = 1.0 / math.sqrt(length)
    cosine = (jnp.cos(angles) * factor).astype(BF16)
    sine = (jnp.sin(angles) * factor).astype(BF16)
    return cosine, sine


def fill_tables(cos_ref, sin_ref, rows_ref, cols_ref):
    n = cos_ref.shape[0]
    cosine = cos_ref[...]
    sine = sin_ref[...]
    rows_ref[:n, :n] = cosine
    rows_ref[:n, n:] = sine
    rows_ref[n:, :n] = -sine
    rows_ref[n:, n:] = cosine
    cols_ref[:n, :n] = cosine
    cols_ref[:n, n:] = -sine
    cols_ref[n:, :n] = sine
    cols_ref[n:, n:] = cosine


def frames_kernel(
    core_ref, pos_ref, cnt_ref, coef_ref, own_ref, right_ref, below_ref, corner_ref, beyond_ref,
    amp_ref, modes_ref, cos_ref, sin_ref,
    keep_ref, give_ref, grads_ref, t_own_ref, t_right_ref, t_below_ref, t_corner_ref,
    ext_ref, tot_ref, probe_ref, exit_ref, rows_ref, cols_ref, stack_ref, side_ref, wide_ref,
    in_sem, out_sem,
):
    frames, n = amp_ref.shape[0], amp_ref.shape[1]
    modes = modes_ref.shape[0]
    lanes = n // 128
    is_first = core_ref[0] == 0

    def quarter(ref, a, b, lane):
        return ref.at[:, b + lane, pl.ds(a, n), :]

    def strip(ref, lane):
        return ref.at[:, :, pl.ds(lane * 128, 128)]

    def load(i, src, a, b):
        return [
            pltpu.make_async_copy(strip(src, lane), quarter(ext_ref, a, b, lane), in_sem.at[i * lanes + lane])
            for lane in range(lanes)
        ]

    loads = load(0, own_ref, 0, 0) + load(1, right_ref, 0, lanes) + load(2, below_ref, n, 0)
    for copy in loads:
        copy.start()

    @pl.when(is_first)
    def _():
        for copy in load(3, beyond_ref, n, lanes):
            copy.start()

    @pl.when(jnp.logical_not(is_first))
    def _():
        for copy in load(3, corner_ref, n, lanes):
            copy.start()

    fill_tables(cos_ref, sin_ref, rows_ref, cols_ref)

    def clear(t, carry):
        at = pl.ds(pl.multiple_of(t * 32, 32), 32)
        for q in range(3):
            for lane in range(2 * lanes):
                tot_ref[q, lane, at, :] = jnp.zeros((32, 128), F32)
        return carry

    lax.fori_loop(0, 2 * n // 32, clear, 0)
    offsets = []
    for f in range(frames):
        r, c = pos_ref[f, 0] & (n - 1), pos_ref[f, 1] & (n - 1)
        offsets.append((r, c >> 7, c & 127))
    weights = [
        [jnp.where(f < cnt_ref[0], coef_ref[f, k], 0.0) for k in range(modes)] for f in range(frames)
    ]
    column = lax.broadcasted_iota(jnp.int32, (ROWS, 128), 1)
    for copy in loads + load(3, corner_ref, n, lanes):
        copy.wait()

    def patch_rows(f, plane, b):
        r, tile, shift = offsets[f]
        at = pl.ds(r + b * ROWS, ROWS)
        back = (128 - shift) & 127
        turned = [pltpu.roll(ext_ref[plane, tile + t, at, :], back, 1) for t in range(lanes + 1)]
        return [jnp.where(column < 128 - shift, turned[t], turned[t + 1]) for t in range(lanes)]

    def start(b, carry):
        at = pl.ds(pl.multiple_of(b * ROWS, ROWS), ROWS)
        at_imag = pl.ds(pl.multiple_of(n + b * ROWS, ROWS), ROWS)
        for f in range(frames):
            reals = patch_rows(f, 0, b)
            imags = patch_rows(f, 1, b)
            for lane in range(lanes):
                col = slice(lane * 128, lane * 128 + 128)
                col_f = slice(f * n + lane * 128, f * n + lane * 128 + 128)
                o_re = reals[lane]
                o_im = imags[lane]
                grads_ref[f, 0, at, col] = o_re
                grads_ref[f, 1, at, col] = o_im
                p_re = weights[f][0] * modes_ref[0, 0, at, col]
                p_im = weights[f][0] * modes_ref[0, 1, at, col]
                for k in range(1, modes):
                    p_re = p_re + weights[f][k] * modes_ref[k, 0, at, col]
                    p_im = p_im + weights[f][k] * modes_ref[k, 1, at, col]
                probe_ref[f, 0, at, col] = p_re
                probe_ref[f, 1, at, col] = p_im
                e_re = p_re * o_re - p_im * o_im
                e_im = p_re * o_im + p_im * o_re
                exit_ref[f, 0, at, col] = e_re
                exit_ref[f, 1, at, col] = e_im
                stack_ref[at, col_f] = e_re.astype(BF16)
                stack_ref[at_imag, col_f] = e_im.astype(BF16)
        return carry

    lax.fori_loop(0, n // ROWS, start, 0)

    def transform(first_ref, second_ref):
        for f in range(frames):
            cols = slice(f * n, (f + 1) * n)
            for h in range(2):
                half = jnp.dot(
                    first_ref[h * n : (h + 1) * n, :], stack_ref[:, cols], preferred_element_type=F32
                )
                side_ref[cols, h * n : (h + 1) * n] = half.astype(BF16)
        for f in range(frames):
            cols = slice(f * n, (f + 1) * n)
            wide_ref[cols, :] = jnp.dot(side_ref[cols, :], second_ref[...], preferred_element_type=F32)

    transform(rows_ref, cols_ref)

    def scale(b, carry):
        at = pl.ds(pl.multiple_of(b * ROWS, ROWS), ROWS)
        at_imag = pl.ds(pl.multiple_of(n + b * ROWS, ROWS), ROWS)
        for f in range(frames):
            at_f = pl.ds(pl.multiple_of(f * n + b * ROWS, ROWS), ROWS)
            far_re = wide_ref[at_f, :n]
            far_im = wide_ref[at_f, n:]
            inverse = jnp.minimum(lax.rsqrt(far_re * far_re + far_im * far_im), 2.0)
            factor = amp_ref[f, at, :].astype(F32) * inverse
            stack_ref[at, f * n : (f + 1) * n] = (far_re * factor).astype(BF16)
            stack_ref[at_imag, f * n : (f + 1) * n] = (far_im * factor).astype(BF16)
        return carry

    lax.fori_loop(0, n // ROWS, scale, 0)
    transform(cols_ref, rows_ref)

    def place(b, carry):
        at = pl.ds(pl.multiple_of(b * ROWS, ROWS), ROWS)
        for f in range(frames):
            r, tile, shift = offsets[f]
            rows = pl.ds(r + b * ROWS, ROWS)
            at_f = pl.ds(pl.multiple_of(f * n + b * ROWS, ROWS), ROWS)
            parts = [[], [], []]
            for lane in range(lanes):
                col = slice(lane * 128, lane * 128 + 128)
                col_im = slice(n + lane * 128, n + lane * 128 + 128)
                d_re = wide_ref[at_f, col] - exit_ref[f, 0, at, col]
                d_im = wide_ref[at_f, col_im] - exit_ref[f, 1, at, col]
                wide_ref[at_f, col] = d_re
                wide_ref[at_f, col_im] = d_im
                p_re = probe_ref[f, 0, at, col]
                p_im = probe_ref[f, 1, at, col]
                parts[0].append(pltpu.roll(p_re * d_re + p_im * d_im, shift, 1))
                parts[1].append(pltpu.roll(p_re * d_im - p_im * d_re, shift, 1))
                parts[2].append(pltpu.roll(p_re * p_re + p_im * p_im, shift, 1))
            for q in range(3):
                for t in range(lanes + 1):
                    before = parts[q][t - 1] if t > 0 else 0.0
                    after = parts[q][t] if t < lanes else 0.0
                    value = jnp.where(column < shift, before, after)
                    tot_ref[q, tile + t, rows, :] = tot_ref[q, tile + t, rows, :] + value
        return carry

    lax.fori_loop(0, n // ROWS, place, 0)
    stores = []
    for i, (dst, a, b) in enumerate(
        ((t_corner_ref, n, lanes), (t_right_ref, 0, lanes), (t_below_ref, n, 0), (t_own_ref, 0, 0))
    ):
        for lane in range(lanes):
            stores.append(
                pltpu.make_async_copy(
                    quarter(tot_ref, a, b, lane), strip(dst, lane), out_sem.at[i * lanes + lane]
                )
            )
    for store in stores:
        store.start()

    def finish(b, carry):
        at = pl.ds(pl.multiple_of(b * 16, 16), 16)
        for lane in range(lanes):
            col = slice(lane * 128, lane * 128 + 128)
            col_im = slice(n + lane * 128, n + lane * 128 + 128)
            slopes = []
            for f in range(frames):
                at_f = pl.ds(pl.multiple_of(f * n + b * 16, 16), 16)
                d_re = wide_ref[at_f, col]
                d_im = wide_ref[at_f, col_im]
                o_re = grads_ref[f, 0, at, col]
                o_im = grads_ref[f, 1, at, col]
                g_re = o_re * d_re + o_im * d_im
                g_im = o_re * d_im - o_im * d_re
                grads_ref[f, 0, at, col] = g_re
                grads_ref[f, 1, at, col] = g_im
                slopes.append((jnp.where(is_first, g_re, g_im), jnp.where(is_first, g_im, g_re)))
            for k in range(modes):
                keep = weights[0][k] * slopes[0][0]
                give = weights[0][k] * slopes[0][1]
                for f in range(1, frames):
                    keep = keep + weights[f][k] * slopes[f][0]
                    give = give + weights[f][k] * slopes[f][1]
                for i in range(2):
                    tile = (2 * b + i) * lanes + lane
                    keep_ref[tile, k] = keep[8 * i : 8 * i + 8]
                    give_ref[tile, k] = give[8 * i : 8 * i + 8]
        return carry

    lax.fori_loop(0, n // 16, finish, 0)
    for store in stores:
        store.wait()


def run_frames(core, positions, count, coefficients, blocks, amplitudes, modes, tables):
    frames, n = amplitudes.shape[0], amplitudes.shape[1]
    k = modes.shape[0]
    tiles = n * n // 1024
    smem = pl.BlockSpec(memory_space=pltpu.SMEM)
    vmem = pl.BlockSpec(memory_space=pltpu.VMEM)
    hbm = pl.BlockSpec(memory_space=pl.ANY)
    piece = jax.ShapeDtypeStruct((tiles, k, 8, 128), F32)
    quarter = jax.ShapeDtypeStruct((3, n, n), F32)
    return pl.pallas_call(
        frames_kernel,
        out_shape=(piece, piece, jax.ShapeDtypeStruct((frames, 2, n, n), F32)) + (quarter,) * 4,
        in_specs=[smem] * 4 + [hbm] * 5 + [vmem] * 4,
        out_specs=(vmem,) * 3 + (hbm,) * 4,
        scratch_shapes=[
            pltpu.VMEM((2, 2 * n // 128, 2 * n, 128), F32),
            pltpu.VMEM((3, 2 * n // 128, 2 * n, 128), F32),
            pltpu.VMEM((frames, 2, n, n), F32),
            pltpu.VMEM((frames, 2, n, n), F32),
            pltpu.VMEM((2 * n, 2 * n), BF16),
            pltpu.VMEM((2 * n, 2 * n), BF16),
            pltpu.VMEM((2 * n, frames * n), BF16),
            pltpu.VMEM((frames * n, 2 * n), BF16),
            pltpu.VMEM((frames * n, 2 * n), F32),
            pltpu.SemaphoreType.DMA((4 * n // 128,)),
            pltpu.SemaphoreType.DMA((4 * n // 128,)),
        ],
        name="frames",
    )(core, positions, count, coefficients, *blocks, amplitudes, modes, *tables)


def spread_kernel(got_ref, out_ref):
    total = jnp.sum(got_ref[...], axis=0)
    out_ref[...] = jnp.broadcast_to(total[None], out_ref.shape)


def run_spread(got):
    vmem = pl.BlockSpec(memory_space=pltpu.VMEM)
    return pl.pallas_call(
        spread_kernel,
        out_shape=jax.ShapeDtypeStruct(got.shape, F32),
        in_specs=[vmem],
        out_specs=vmem,
        name="spread",
    )(got)


def total_of(acc):
    across = jnp.sum(jnp.sum(acc, axis=0, keepdims=True), axis=1, keepdims=True)
    return jnp.broadcast_to(across, acc.shape)


def modes_kernel(
    core_ref, cnt_ref, coef_ref, mine_ref, other_ref, old_ref, grads_ref, new_ref, out_coef_ref, raised_ref,
    *, root_total,
):
    modes, n = old_ref.shape[0], old_ref.shape[2]
    frames = grads_ref.shape[0]
    pixels = n * n
    is_first = core_ref[0] == 0
    lanes = n // 128
    pairs = [(i, j) for j in range(modes) for i in range(j)]
    zero = jnp.zeros((8, 128), F32)

    def lift(t, acc):
        acc = list(acc)
        at = pl.ds(pl.multiple_of(t * 8, 8), 8)
        for lane in range(lanes):
            col = slice(lane * 128, lane * 128 + 128)
            tile = t * lanes + lane
            re, im = [], []
            for k in range(modes):
                mine = mine_ref[tile, k]
                other = other_ref[tile, k]
                s_re = jnp.where(is_first, mine, other)
                s_im = jnp.where(is_first, other, mine)
                re.append(old_ref[k, 0, at, col] + s_re * (1.0 / root_total))
                im.append(old_ref[k, 1, at, col] + s_im * (1.0 / root_total))
                raised_ref[k, 0, at, col] = re[k]
                raised_ref[k, 1, at, col] = im[k]
            for k in range(modes):
                acc[k] = acc[k] + (re[k] * re[k] + im[k] * im[k])
            for p, (i, j) in enumerate(pairs):
                acc[modes + 2 * p] = acc[modes + 2 * p] + (re[i] * re[j] + im[i] * im[j])
                acc[modes + 2 * p + 1] = acc[modes + 2 * p + 1] + (re[i] * im[j] - im[i] * re[j])
        return tuple(acc)

    acc = lax.fori_loop(0, n // 8, lift, (zero,) * (modes + 2 * len(pairs)))
    gram = [total_of(a) * (1.0 / pixels) for a in acc]
    upper = {}
    inverse = []
    for j in range(modes):
        for i in range(j):
            p = pairs.index((i, j))
            s_re = gram[modes + 2 * p]
            s_im = gram[modes + 2 * p + 1]
            for k in range(i):
                a_re, a_im = upper[k, i]
                b_re, b_im = upper[k, j]
                s_re = s_re - (a_re * b_re + a_im * b_im)
                s_im = s_im - (a_re * b_im - a_im * b_re)
            upper[i, j] = (s_re * inverse[i], s_im * inverse[i])
        diagonal = gram[j]
        for k in range(j):
            a_re, a_im = upper[k, j]
            diagonal = diagonal - (a_re * a_re + a_im * a_im)
        inverse.append(1.0 / jnp.sqrt(diagonal))

    def solve(t, acc):
        acc = list(acc)
        at = pl.ds(pl.multiple_of(t * 8, 8), 8)
        for lane in range(lanes):
            col = slice(lane * 128, lane * 128 + 128)
            basis = []
            for j in range(modes):
                v_re = raised_ref[j, 0, at, col]
                v_im = raised_ref[j, 1, at, col]
                for i in range(j):
                    r_re, r_im = upper[i, j]
                    q_re, q_im = basis[i]
                    v_re = v_re - (r_re * q_re - r_im * q_im)
                    v_im = v_im - (r_re * q_im + r_im * q_re)
                basis.append((v_re * inverse[j], v_im * inverse[j]))
                new_ref[j, 0, at, col] = basis[j][0]
                new_ref[j, 1, at, col] = basis[j][1]
            for j in range(modes):
                o_re = old_ref[j, 0, at, col]
                o_im = old_ref[j, 1, at, col]
                for k in range(modes):
                    s = j * modes + k
                    acc[s] = acc[s] + (basis[k][0] * o_re + basis[k][1] * o_im)
            for f in range(frames):
                g_re = grads_ref[f, 0, at, col]
                g_im = grads_ref[f, 1, at, col]
                for k in range(modes):
                    s = (modes + f) * modes + k
                    acc[s] = acc[s] + (basis[k][0] * g_re + basis[k][1] * g_im)
        return tuple(acc)

    acc = lax.fori_loop(0, n // 8, solve, (zero,) * ((modes + frames) * modes))
    dots = [jnp.sum(a) * (1.0 / pixels) for a in acc]
    for f in range(frames):
        for k in range(modes):
            value = 0.5 * dots[(modes + f) * modes + k]
            for j in range(modes):
                value = value + coef_ref[f, j] * dots[j * modes + k]
            out_coef_ref[f, k] = jnp.where(f < cnt_ref[0], value, coef_ref[f, k])


def run_modes(core, count, coefficients, mine, other, old, grads, root_total):
    smem = pl.BlockSpec(memory_space=pltpu.SMEM)
    vmem = pl.BlockSpec(memory_space=pltpu.VMEM)
    return pl.pallas_call(
        functools.partial(modes_kernel, root_total=root_total),
        out_shape=(
            jax.ShapeDtypeStruct(old.shape, F32),
            jax.ShapeDtypeStruct(coefficients.shape, F32),
        ),
        in_specs=[smem] * 3 + [vmem] * 4,
        out_specs=(vmem, smem),
        scratch_shapes=[pltpu.VMEM(old.shape, F32)],
        name="modes",
    )(core, count, coefficients, mine, other, old, grads)


def moves(scans, cols, down, over, odd_from=None):
    pairs = []
    for s in range(scans):
        for c in range(cols):
            inside = 0 <= s + down < scans and 0 <= c + over < cols
            if inside and (odd_from is None or s % 2 == odd_from):
                pairs.append((s * cols + c, (s + down) * cols + c + over))
    return pairs


def on_device(object_field, amplitudes, positions, frame_count, coefficients, probe_modes):
    frames, length = amplitudes.shape[0], amplitudes.shape[1]
    cols = lax.axis_size("y")
    scans = lax.axis_size(SCAN)
    root_total = math.sqrt(frames * scans * cols)
    core = lax.axis_index("core").astype(jnp.int32).reshape(1)
    swap = [(0, 1), (1, 0)]

    def widen(block):
        right = lax.ppermute(block, ALL, moves(scans, cols, 0, -1))
        corner = lax.ppermute(block, ALL, moves(scans, cols, -1, -1, 0))
        below = lax.ppermute(block, ALL, moves(scans, cols, -1, 0))
        beyond = lax.ppermute(right, "core", [(1, 0)])
        return [block, right, below, corner, beyond]

    tables = make_tables(length)
    blocks = widen(object_field)
    for iteration in range(ITERS):
        keep, give, grads, t_own, t_right, t_below, t_corner = run_frames(
            core, positions, frame_count, coefficients, blocks, amplitudes, probe_modes, tables
        )
        joined = t_right + lax.ppermute(t_corner, "core", [(0, 1)])
        kept = keep + lax.ppermute(give, "core", swap)
        arrived = lax.ppermute(joined, ALL, moves(scans, cols, 0, 1))
        crossed = lax.ppermute(t_corner, ALL, moves(scans, cols, 1, 1, 1))
        lowered = lax.ppermute(t_below, ALL, moves(scans, cols, 1, 0))
        got = lax.all_to_all(kept, CHIPS, split_axis=0, concat_axis=0, tiled=True)
        settled = t_own + arrived + lowered + crossed
        object_field = object_field + settled[:2] / (settled[2] + 1.0)
        if iteration + 1 < ITERS:
            blocks = widen(object_field)
            got, object_field = lax.optimization_barrier((got, object_field))
        spread = run_spread(got)
        mine = lax.all_to_all(spread, CHIPS, split_axis=0, concat_axis=0, tiled=True)
        other = lax.ppermute(mine, "core", swap)
        probe_modes, coefficients = run_modes(
            core, frame_count, coefficients, mine, other, probe_modes, grads, root_total
        )
    return (object_field, probe_modes, coefficients)


def solution(mesh):
    scans, cols = mesh.shape["scan"], mesh.shape["col"]
    fine = Mesh(np.asarray(mesh.devices).reshape(4, scans // 8, 2, cols), ALL)
    placed = (
        P(None, SCAN, "y"),
        P(ALL, None, None),
        P(ALL, None),
        P(ALL),
        P(ALL, None),
        P(),
    )
    return jax.shard_map(
        on_device,
        mesh=fine,
        in_specs=placed,
        out_specs=(P(None, SCAN, "y"), P(), P(ALL, None)),
        check_vma=False,
    )
```

```python
import functools
import math

import jax
import jax.numpy as jnp
import numpy as np
from jax import lax
from jax.experimental import pallas as pl
from jax.experimental.pallas import tpu as pltpu
from jax.sharding import Mesh
from jax.sharding import PartitionSpec as P

ITERS = 2
F32 = jnp.float32
BF16 = jnp.bfloat16
CHIPS = ("z", "x", "y")
SCAN = ("z", "x", "core")
ALL = ("z", "x", "core", "y")
ROWS = 32


def make_tables(length):
    indices = jnp.arange(length, dtype=jnp.int32)
    phases = indices[:, None] * indices[None, :] % length
    angles = phases.astype(F32) * (2.0 * math.pi / length)
    factor = 1.0 / math.sqrt(length)
    cosine = (jnp.cos(angles) * factor).astype(BF16)
    sine = (jnp.sin(angles) * factor).astype(BF16)
    return cosine, sine


def fill_tables(cos_ref, sin_ref, rows_ref, cols_ref):
    n = cos_ref.shape[0]
    cosine = cos_ref[...]
    sine = sin_ref[...]
    rows_ref[:n, :n] = cosine
    rows_ref[:n, n:] = sine
    rows_ref[n:, :n] = -sine
    rows_ref[n:, n:] = cosine
    cols_ref[:n, :n] = cosine
    cols_ref[:n, n:] = -sine
    cols_ref[n:, :n] = sine
    cols_ref[n:, n:] = cosine


def frames_kernel(
    core_ref, pos_ref, cnt_ref, coef_ref, own_ref, right_ref, below_ref, corner_ref,
    amp_ref, modes_ref, cos_ref, sin_ref,
    keep_ref, give_ref, grads_ref, t_own_ref, t_right_ref, t_below_ref, t_corner_ref,
    ext_ref, tot_ref, probe_ref, exit_ref, rows_ref, cols_ref, stack_ref, side_ref, wide_ref,
    in_sem, out_sem,
):
    frames, n = amp_ref.shape[0], amp_ref.shape[1]
    modes = modes_ref.shape[0]
    lanes = n // 128
    is_first = core_ref[0] == 0

    def quarter(ref, a, b, lane):
        return ref.at[:, b + lane, pl.ds(a, n), :]

    def strip(ref, lane):
        return ref.at[:, :, pl.ds(lane * 128, 128)]

    def load(i, src, a, b):
        return [
            pltpu.make_async_copy(strip(src, lane), quarter(ext_ref, a, b, lane), in_sem.at[i * lanes + lane])
            for lane in range(lanes)
        ]

    loads = load(0, own_ref, 0, 0) + load(1, right_ref, 0, lanes)
    loads += load(2, below_ref, n, 0) + load(3, corner_ref, n, lanes)
    for copy in loads:
        copy.start()
    fill_tables(cos_ref, sin_ref, rows_ref, cols_ref)

    def clear(t, carry):
        at = pl.ds(pl.multiple_of(t * 32, 32), 32)
        for q in range(3):
            for lane in range(2 * lanes):
                tot_ref[q, lane, at, :] = jnp.zeros((32, 128), F32)
        return carry

    lax.fori_loop(0, 2 * n // 32, clear, 0)
    offsets = []
    for f in range(frames):
        r, c = pos_ref[f, 0] & (n - 1), pos_ref[f, 1] & (n - 1)
        offsets.append((r, c >> 7, c & 127))
    weights = [
        [jnp.where(f < cnt_ref[0], coef_ref[f, k], 0.0) for k in range(modes)] for f in range(frames)
    ]
    column = lax.broadcasted_iota(jnp.int32, (ROWS, 128), 1)
    for copy in loads:
        copy.wait()

    def patch_rows(f, plane, b):
        r, tile, shift = offsets[f]
        at = pl.ds(r + b * ROWS, ROWS)
        back = (128 - shift) & 127
        turned = [pltpu.roll(ext_ref[plane, tile + t, at, :], back, 1) for t in range(lanes + 1)]
        return [jnp.where(column < 128 - shift, turned[t], turned[t + 1]) for t in range(lanes)]

    def start(b, carry):
        at = pl.ds(pl.multiple_of(b * ROWS, ROWS), ROWS)
        at_imag = pl.ds(pl.multiple_of(n + b * ROWS, ROWS), ROWS)
        for f in range(frames):
            reals = patch_rows(f, 0, b)
            imags = patch_rows(f, 1, b)
            for lane in range(lanes):
                col = slice(lane * 128, lane * 128 + 128)
                col_f = slice(f * n + lane * 128, f * n + lane * 128 + 128)
                o_re = reals[lane]
                o_im = imags[lane]
                grads_ref[f, 0, at, col] = o_re
                grads_ref[f, 1, at, col] = o_im
                p_re = weights[f][0] * modes_ref[0, 0, at, col]
                p_im = weights[f][0] * modes_ref[0, 1, at, col]
                for k in range(1, modes):
                    p_re = p_re + weights[f][k] * modes_ref[k, 0, at, col]
                    p_im = p_im + weights[f][k] * modes_ref[k, 1, at, col]
                probe_ref[f, 0, at, col] = p_re
                probe_ref[f, 1, at, col] = p_im
                e_re = p_re * o_re - p_im * o_im
                e_im = p_re * o_im + p_im * o_re
                exit_ref[f, 0, at, col] = e_re
                exit_ref[f, 1, at, col] = e_im
                stack_ref[at, col_f] = e_re.astype(BF16)
                stack_ref[at_imag, col_f] = e_im.astype(BF16)
        return carry

    lax.fori_loop(0, n // ROWS, start, 0)

    def transform(first_ref, second_ref):
        for f in range(frames):
            cols = slice(f * n, (f + 1) * n)
            for h in range(2):
                half = jnp.dot(
                    first_ref[h * n : (h + 1) * n, :], stack_ref[:, cols], preferred_element_type=F32
                )
                side_ref[cols, h * n : (h + 1) * n] = half.astype(BF16)
        for f in range(frames):
            cols = slice(f * n, (f + 1) * n)
            wide_ref[cols, :] = jnp.dot(side_ref[cols, :], second_ref[...], preferred_element_type=F32)

    transform(rows_ref, cols_ref)

    def scale(b, carry):
        at = pl.ds(pl.multiple_of(b * ROWS, ROWS), ROWS)
        at_imag = pl.ds(pl.multiple_of(n + b * ROWS, ROWS), ROWS)
        for f in range(frames):
            at_f = pl.ds(pl.multiple_of(f * n + b * ROWS, ROWS), ROWS)
            far_re = wide_ref[at_f, :n]
            far_im = wide_ref[at_f, n:]
            inverse = jnp.minimum(lax.rsqrt(far_re * far_re + far_im * far_im), 2.0)
            factor = amp_ref[f, at, :].astype(F32) * inverse
            stack_ref[at, f * n : (f + 1) * n] = (far_re * factor).astype(BF16)
            stack_ref[at_imag, f * n : (f + 1) * n] = (far_im * factor).astype(BF16)
        return carry

    lax.fori_loop(0, n // ROWS, scale, 0)
    transform(cols_ref, rows_ref)

    def place(b, carry):
        at = pl.ds(pl.multiple_of(b * ROWS, ROWS), ROWS)
        for f in range(frames):
            r, tile, shift = offsets[f]
            rows = pl.ds(r + b * ROWS, ROWS)
            at_f = pl.ds(pl.multiple_of(f * n + b * ROWS, ROWS), ROWS)
            parts = [[], [], []]
            for lane in range(lanes):
                col = slice(lane * 128, lane * 128 + 128)
                col_im = slice(n + lane * 128, n + lane * 128 + 128)
                d_re = wide_ref[at_f, col] - exit_ref[f, 0, at, col]
                d_im = wide_ref[at_f, col_im] - exit_ref[f, 1, at, col]
                wide_ref[at_f, col] = d_re
                wide_ref[at_f, col_im] = d_im
                p_re = probe_ref[f, 0, at, col]
                p_im = probe_ref[f, 1, at, col]
                parts[0].append(pltpu.roll(p_re * d_re + p_im * d_im, shift, 1))
                parts[1].append(pltpu.roll(p_re * d_im - p_im * d_re, shift, 1))
                parts[2].append(pltpu.roll(p_re * p_re + p_im * p_im, shift, 1))
            for q in range(3):
                for t in range(lanes + 1):
                    before = parts[q][t - 1] if t > 0 else 0.0
                    after = parts[q][t] if t < lanes else 0.0
                    value = jnp.where(column < shift, before, after)
                    tot_ref[q, tile + t, rows, :] = tot_ref[q, tile + t, rows, :] + value
        return carry

    lax.fori_loop(0, n // ROWS, place, 0)
    stores = []
    for i, (dst, a, b) in enumerate(
        ((t_corner_ref, n, lanes), (t_right_ref, 0, lanes), (t_below_ref, n, 0), (t_own_ref, 0, 0))
    ):
        for lane in range(lanes):
            stores.append(
                pltpu.make_async_copy(
                    quarter(tot_ref, a, b, lane), strip(dst, lane), out_sem.at[i * lanes + lane]
                )
            )
    for store in stores:
        store.start()

    def finish(b, carry):
        at = pl.ds(pl.multiple_of(b * 16, 16), 16)
        for lane in range(lanes):
            col = slice(lane * 128, lane * 128 + 128)
            col_im = slice(n + lane * 128, n + lane * 128 + 128)
            slopes = []
            for f in range(frames):
                at_f = pl.ds(pl.multiple_of(f * n + b * 16, 16), 16)
                d_re = wide_ref[at_f, col]
                d_im = wide_ref[at_f, col_im]
                o_re = grads_ref[f, 0, at, col]
                o_im = grads_ref[f, 1, at, col]
                g_re = o_re * d_re + o_im * d_im
                g_im = o_re * d_im - o_im * d_re
                grads_ref[f, 0, at, col] = g_re
                grads_ref[f, 1, at, col] = g_im
                slopes.append((jnp.where(is_first, g_re, g_im), jnp.where(is_first, g_im, g_re)))
            for k in range(modes):
                keep = weights[0][k] * slopes[0][0]
                give = weights[0][k] * slopes[0][1]
                for f in range(1, frames):
                    keep = keep + weights[f][k] * slopes[f][0]
                    give = give + weights[f][k] * slopes[f][1]
                for i in range(2):
                    tile = (2 * b + i) * lanes + lane
                    keep_ref[tile, k] = keep[8 * i : 8 * i + 8]
                    give_ref[tile, k] = give[8 * i : 8 * i + 8]
        return carry

    lax.fori_loop(0, n // 16, finish, 0)
    for store in stores:
        store.wait()


def run_frames(core, positions, count, coefficients, blocks, amplitudes, modes, tables):
    frames, n = amplitudes.shape[0], amplitudes.shape[1]
    k = modes.shape[0]
    tiles = n * n // 1024
    smem = pl.BlockSpec(memory_space=pltpu.SMEM)
    vmem = pl.BlockSpec(memory_space=pltpu.VMEM)
    hbm = pl.BlockSpec(memory_space=pl.ANY)
    piece = jax.ShapeDtypeStruct((tiles, k, 8, 128), F32)
    quarter = jax.ShapeDtypeStruct((3, n, n), F32)
    return pl.pallas_call(
        frames_kernel,
        out_shape=(piece, piece, jax.ShapeDtypeStruct((frames, 2, n, n), F32)) + (quarter,) * 4,
        in_specs=[smem] * 4 + [hbm] * 4 + [vmem] * 4,
        out_specs=(vmem,) * 3 + (hbm,) * 4,
        scratch_shapes=[
            pltpu.VMEM((2, 2 * n // 128, 2 * n, 128), F32),
            pltpu.VMEM((3, 2 * n // 128, 2 * n, 128), F32),
            pltpu.VMEM((frames, 2, n, n), F32),
            pltpu.VMEM((frames, 2, n, n), F32),
            pltpu.VMEM((2 * n, 2 * n), BF16),
            pltpu.VMEM((2 * n, 2 * n), BF16),
            pltpu.VMEM((2 * n, frames * n), BF16),
            pltpu.VMEM((frames * n, 2 * n), BF16),
            pltpu.VMEM((frames * n, 2 * n), F32),
            pltpu.SemaphoreType.DMA((4 * n // 128,)),
            pltpu.SemaphoreType.DMA((4 * n // 128,)),
        ],
        name="frames",
    )(core, positions, count, coefficients, *blocks, amplitudes, modes, *tables)


def spread_kernel(got_ref, out_ref):
    total = jnp.sum(got_ref[...], axis=0)
    out_ref[...] = jnp.broadcast_to(total[None], out_ref.shape)


def run_spread(got):
    vmem = pl.BlockSpec(memory_space=pltpu.VMEM)
    return pl.pallas_call(
        spread_kernel,
        out_shape=jax.ShapeDtypeStruct(got.shape, F32),
        in_specs=[vmem],
        out_specs=vmem,
        name="spread",
    )(got)


def total_of(acc):
    across = jnp.sum(jnp.sum(acc, axis=0, keepdims=True), axis=1, keepdims=True)
    return jnp.broadcast_to(across, acc.shape)


def modes_kernel(
    core_ref, cnt_ref, coef_ref, mine_ref, other_ref, old_ref, grads_ref, new_ref, out_coef_ref, raised_ref,
    *, root_total,
):
    modes, n = old_ref.shape[0], old_ref.shape[2]
    frames = grads_ref.shape[0]
    pixels = n * n
    is_first = core_ref[0] == 0
    lanes = n // 128
    pairs = [(i, j) for j in range(modes) for i in range(j)]
    zero = jnp.zeros((8, 128), F32)

    def lift(t, acc):
        acc = list(acc)
        at = pl.ds(pl.multiple_of(t * 8, 8), 8)
        for lane in range(lanes):
            col = slice(lane * 128, lane * 128 + 128)
            tile = t * lanes + lane
            re, im = [], []
            for k in range(modes):
                mine = mine_ref[tile, k]
                other = other_ref[tile, k]
                s_re = jnp.where(is_first, mine, other)
                s_im = jnp.where(is_first, other, mine)
                re.append(old_ref[k, 0, at, col] + s_re * (1.0 / root_total))
                im.append(old_ref[k, 1, at, col] + s_im * (1.0 / root_total))
                raised_ref[k, 0, at, col] = re[k]
                raised_ref[k, 1, at, col] = im[k]
            for k in range(modes):
                acc[k] = acc[k] + (re[k] * re[k] + im[k] * im[k])
            for p, (i, j) in enumerate(pairs):
                acc[modes + 2 * p] = acc[modes + 2 * p] + (re[i] * re[j] + im[i] * im[j])
                acc[modes + 2 * p + 1] = acc[modes + 2 * p + 1] + (re[i] * im[j] - im[i] * re[j])
        return tuple(acc)

    acc = lax.fori_loop(0, n // 8, lift, (zero,) * (modes + 2 * len(pairs)))
    gram = [total_of(a) * (1.0 / pixels) for a in acc]
    upper = {}
    inverse = []
    for j in range(modes):
        for i in range(j):
            p = pairs.index((i, j))
            s_re = gram[modes + 2 * p]
            s_im = gram[modes + 2 * p + 1]
            for k in range(i):
                a_re, a_im = upper[k, i]
                b_re, b_im = upper[k, j]
                s_re = s_re - (a_re * b_re + a_im * b_im)
                s_im = s_im - (a_re * b_im - a_im * b_re)
            upper[i, j] = (s_re * inverse[i], s_im * inverse[i])
        diagonal = gram[j]
        for k in range(j):
            a_re, a_im = upper[k, j]
            diagonal = diagonal - (a_re * a_re + a_im * a_im)
        inverse.append(1.0 / jnp.sqrt(diagonal))

    def solve(t, acc):
        acc = list(acc)
        at = pl.ds(pl.multiple_of(t * 8, 8), 8)
        for lane in range(lanes):
            col = slice(lane * 128, lane * 128 + 128)
            basis = []
            for j in range(modes):
                v_re = raised_ref[j, 0, at, col]
                v_im = raised_ref[j, 1, at, col]
                for i in range(j):
                    r_re, r_im = upper[i, j]
                    q_re, q_im = basis[i]
                    v_re = v_re - (r_re * q_re - r_im * q_im)
                    v_im = v_im - (r_re * q_im + r_im * q_re)
                basis.append((v_re * inverse[j], v_im * inverse[j]))
                new_ref[j, 0, at, col] = basis[j][0]
                new_ref[j, 1, at, col] = basis[j][1]
            for j in range(modes):
                o_re = old_ref[j, 0, at, col]
                o_im = old_ref[j, 1, at, col]
                for k in range(modes):
                    s = j * modes + k
                    acc[s] = acc[s] + (basis[k][0] * o_re + basis[k][1] * o_im)
            for f in range(frames):
                g_re = grads_ref[f, 0, at, col]
                g_im = grads_ref[f, 1, at, col]
                for k in range(modes):
                    s = (modes + f) * modes + k
                    acc[s] = acc[s] + (basis[k][0] * g_re + basis[k][1] * g_im)
        return tuple(acc)

    acc = lax.fori_loop(0, n // 8, solve, (zero,) * ((modes + frames) * modes))
    dots = [jnp.sum(a) * (1.0 / pixels) for a in acc]
    for f in range(frames):
        for k in range(modes):
            value = 0.5 * dots[(modes + f) * modes + k]
            for j in range(modes):
                value = value + coef_ref[f, j] * dots[j * modes + k]
            out_coef_ref[f, k] = jnp.where(f < cnt_ref[0], value, coef_ref[f, k])


def run_modes(core, count, coefficients, mine, other, old, grads, root_total):
    smem = pl.BlockSpec(memory_space=pltpu.SMEM)
    vmem = pl.BlockSpec(memory_space=pltpu.VMEM)
    return pl.pallas_call(
        functools.partial(modes_kernel, root_total=root_total),
        out_shape=(
            jax.ShapeDtypeStruct(old.shape, F32),
            jax.ShapeDtypeStruct(coefficients.shape, F32),
        ),
        in_specs=[smem] * 3 + [vmem] * 4,
        out_specs=(vmem, smem),
        scratch_shapes=[pltpu.VMEM(old.shape, F32)],
        name="modes",
    )(core, count, coefficients, mine, other, old, grads)


def moves(scans, cols, down, over):
    pairs = []
    for s in range(scans):
        for c in range(cols):
            if 0 <= s + down < scans and 0 <= c + over < cols:
                pairs.append((s * cols + c, (s + down) * cols + c + over))
    return pairs


def on_device(object_field, amplitudes, positions, frame_count, coefficients, probe_modes):
    frames, length = amplitudes.shape[0], amplitudes.shape[1]
    cols = lax.axis_size("y")
    scans = lax.axis_size(SCAN)
    root_total = math.sqrt(frames * scans * cols)
    core = lax.axis_index("core").astype(jnp.int32).reshape(1)
    swap = [(0, 1), (1, 0)]

    def widen(block):
        right = lax.ppermute(block, ALL, moves(scans, cols, 0, -1))
        below = lax.ppermute(block, ALL, moves(scans, cols, -1, 0))
        corner = lax.ppermute(right, ALL, moves(scans, cols, -1, 0))
        return [block, right, below, corner]

    tables = lax.optimization_barrier(make_tables(length))
    blocks = widen(object_field)
    for iteration in range(ITERS):
        keep, give, grads, t_own, t_right, t_below, t_corner = run_frames(
            core, positions, frame_count, coefficients, blocks, amplitudes, probe_modes, tables
        )
        crossed = lax.ppermute(t_corner, ALL, moves(scans, cols, 1, 0))
        joined = t_right + crossed
        kept = keep + lax.ppermute(give, "core", swap)
        arrived = lax.ppermute(joined, ALL, moves(scans, cols, 0, 1))
        lowered = lax.ppermute(t_below, ALL, moves(scans, cols, 1, 0))
        got = lax.all_to_all(kept, CHIPS, split_axis=0, concat_axis=0, tiled=True)
        settled = t_own + arrived + lowered
        object_field = object_field + settled[:2] / (settled[2] + 1.0)
        if iteration + 1 < ITERS:
            blocks = widen(object_field)
        spread = run_spread(got)
        mine = lax.all_to_all(spread, CHIPS, split_axis=0, concat_axis=0, tiled=True)
        other = lax.ppermute(mine, "core", swap)
        probe_modes, coefficients = run_modes(
            core, frame_count, coefficients, mine, other, probe_modes, grads, root_total
        )
    return (object_field, probe_modes, coefficients)


def solution(mesh):
    scans, cols = mesh.shape["scan"], mesh.shape["col"]
    fine = Mesh(np.asarray(mesh.devices).reshape(4, scans // 8, 2, cols), ALL)
    placed = (
        P(None, SCAN, "y"),
        P(ALL, None, None),
        P(ALL, None),
        P(ALL),
        P(ALL, None),
        P(),
    )
    return jax.shard_map(
        on_device,
        mesh=fine,
        in_specs=placed,
        out_specs=(P(None, SCAN, "y"), P(), P(ALL, None)),
        check_vma=False,
    )
```

```python
import functools
import math

import jax
import jax.numpy as jnp
import numpy as np
from jax import lax
from jax.experimental import pallas as pl
from jax.experimental.pallas import tpu as pltpu
from jax.sharding import Mesh
from jax.sharding import PartitionSpec as P

ITERS = 2
F32 = jnp.float32
BF16 = jnp.bfloat16
CHIPS = ("z", "x", "y")
SCAN = ("z", "x", "core")
ALL = ("z", "x", "core", "y")
ROWS = 32
CHUNKS = 4
SMALL = pltpu.CompilerParams(vmem_limit_bytes=32 * 1024 * 1024)


def make_tables(length):
    indices = jnp.arange(length, dtype=jnp.int32)
    phases = indices[:, None] * indices[None, :] % length
    angles = phases.astype(F32) * (2.0 * math.pi / length)
    factor = 1.0 / math.sqrt(length)
    cosine = (jnp.cos(angles) * factor).astype(BF16)
    sine = (jnp.sin(angles) * factor).astype(BF16)
    return cosine, sine


def fill_tables(cos_ref, sin_ref, rows_ref, cols_ref):
    n = cos_ref.shape[0]
    cosine = cos_ref[...]
    sine = sin_ref[...]
    rows_ref[:n, :n] = cosine
    rows_ref[:n, n:] = sine
    rows_ref[n:, :n] = -sine
    rows_ref[n:, n:] = cosine
    cols_ref[:n, :n] = cosine
    cols_ref[:n, n:] = -sine
    cols_ref[n:, :n] = sine
    cols_ref[n:, n:] = cosine


def near(x):
    return pltpu.with_memory_space_constraint(x, pltpu.VMEM)


def far(x):
    return pltpu.with_memory_space_constraint(x, pltpu.HBM)


def frames_kernel(
    core_ref, pos_ref, cnt_ref, coef_ref, own_ref, right_ref, below_ref, corner_ref,
    amp_hbm, modes_in, cos_ref, sin_ref,
    keep_ref, give_ref, grads_hbm, t_own_ref, t_right_ref, t_below_ref, t_corner_ref,
    ext_ref, tot_ref, probe_ref, exit_ref, rows_ref, cols_ref, stack_ref, side_ref, wide_ref,
    amp_ref, grads_ref, modes_ref, in_sem, out_sem, side_sem, *, staged,
):
    frames, n = amp_ref.shape[0], amp_ref.shape[1]
    modes = modes_in.shape[0]
    amp_load = pltpu.make_async_copy(amp_hbm, amp_ref, side_sem.at[0])
    modes_load = pltpu.make_async_copy(modes_in, modes_ref, side_sem.at[1])
    if staged:
        modes_load.start()
    else:
        modes_ref = modes_in
    lanes = n // 128
    is_first = core_ref[0] == 0

    def quarter(ref, a, b, lane):
        return ref.at[:, b + lane, pl.ds(a, n), :]

    def strip(ref, lane):
        return ref.at[:, :, pl.ds(lane * 128, 128)]

    def load(i, src, a, b):
        return [
            pltpu.make_async_copy(strip(src, lane), quarter(ext_ref, a, b, lane), in_sem.at[i * lanes + lane])
            for lane in range(lanes)
        ]

    loads = load(0, own_ref, 0, 0) + load(1, right_ref, 0, lanes)
    loads += load(2, below_ref, n, 0) + load(3, corner_ref, n, lanes)
    for copy in loads:
        copy.start()
    amp_load.start()
    fill_tables(cos_ref, sin_ref, rows_ref, cols_ref)

    def clear(t, carry):
        at = pl.ds(pl.multiple_of(t * 32, 32), 32)
        for q in range(3):
            for lane in range(2 * lanes):
                tot_ref[q, lane, at, :] = jnp.zeros((32, 128), F32)
        return carry

    lax.fori_loop(0, 2 * n // 32, clear, 0)
    offsets = []
    for f in range(frames):
        r, c = pos_ref[f, 0] & (n - 1), pos_ref[f, 1] & (n - 1)
        offsets.append((r, c >> 7, c & 127))
    weights = [
        [jnp.where(f < cnt_ref[0], coef_ref[f, k], 0.0) for k in range(modes)] for f in range(frames)
    ]
    column = lax.broadcasted_iota(jnp.int32, (ROWS, 128), 1)
    for copy in loads:
        copy.wait()
    if staged:
        modes_load.wait()

    def patch_rows(f, plane, b):
        r, tile, shift = offsets[f]
        at = pl.ds(r + b * ROWS, ROWS)
        back = (128 - shift) & 127
        turned = [pltpu.roll(ext_ref[plane, tile + t, at, :], back, 1) for t in range(lanes + 1)]
        return [jnp.where(column < 128 - shift, turned[t], turned[t + 1]) for t in range(lanes)]

    def start(b, carry):
        at = pl.ds(pl.multiple_of(b * ROWS, ROWS), ROWS)
        at_imag = pl.ds(pl.multiple_of(n + b * ROWS, ROWS), ROWS)
        for f in range(frames):
            reals = patch_rows(f, 0, b)
            imags = patch_rows(f, 1, b)
            for lane in range(lanes):
                col = slice(lane * 128, lane * 128 + 128)
                col_f = slice(f * n + lane * 128, f * n + lane * 128 + 128)
                o_re = reals[lane]
                o_im = imags[lane]
                grads_ref[f, 0, at, col] = o_re
                grads_ref[f, 1, at, col] = o_im
                p_re = weights[f][0] * modes_ref[0, 0, at, col]
                p_im = weights[f][0] * modes_ref[0, 1, at, col]
                for k in range(1, modes):
                    p_re = p_re + weights[f][k] * modes_ref[k, 0, at, col]
                    p_im = p_im + weights[f][k] * modes_ref[k, 1, at, col]
                probe_ref[f, 0, at, col] = p_re
                probe_ref[f, 1, at, col] = p_im
                e_re = p_re * o_re - p_im * o_im
                e_im = p_re * o_im + p_im * o_re
                exit_ref[f, 0, at, col] = e_re
                exit_ref[f, 1, at, col] = e_im
                stack_ref[at, col_f] = e_re.astype(BF16)
                stack_ref[at_imag, col_f] = e_im.astype(BF16)
        return carry

    lax.fori_loop(0, n // ROWS, start, 0)

    def transform(first_ref, second_ref):
        for f in range(frames):
            cols = slice(f * n, (f + 1) * n)
            for h in range(2):
                half = jnp.dot(
                    first_ref[h * n : (h + 1) * n, :], stack_ref[:, cols], preferred_element_type=F32
                )
                side_ref[cols, h * n : (h + 1) * n] = half.astype(BF16)
        for f in range(frames):
            cols = slice(f * n, (f + 1) * n)
            wide_ref[cols, :] = jnp.dot(side_ref[cols, :], second_ref[...], preferred_element_type=F32)

    transform(rows_ref, cols_ref)
    amp_load.wait()

    def scale(b, carry):
        at = pl.ds(pl.multiple_of(b * ROWS, ROWS), ROWS)
        at_imag = pl.ds(pl.multiple_of(n + b * ROWS, ROWS), ROWS)
        for f in range(frames):
            at_f = pl.ds(pl.multiple_of(f * n + b * ROWS, ROWS), ROWS)
            far_re = wide_ref[at_f, :n]
            far_im = wide_ref[at_f, n:]
            inverse = jnp.minimum(lax.rsqrt(far_re * far_re + far_im * far_im), 2.0)
            factor = amp_ref[f, at, :].astype(F32) * inverse
            stack_ref[at, f * n : (f + 1) * n] = (far_re * factor).astype(BF16)
            stack_ref[at_imag, f * n : (f + 1) * n] = (far_im * factor).astype(BF16)
        return carry

    lax.fori_loop(0, n // ROWS, scale, 0)
    transform(cols_ref, rows_ref)

    def place(b, carry):
        at = pl.ds(pl.multiple_of(b * ROWS, ROWS), ROWS)
        for f in range(frames):
            r, tile, shift = offsets[f]
            rows = pl.ds(r + b * ROWS, ROWS)
            at_f = pl.ds(pl.multiple_of(f * n + b * ROWS, ROWS), ROWS)
            parts = [[], [], []]
            for lane in range(lanes):
                col = slice(lane * 128, lane * 128 + 128)
                col_im = slice(n + lane * 128, n + lane * 128 + 128)
                d_re = wide_ref[at_f, col] - exit_ref[f, 0, at, col]
                d_im = wide_ref[at_f, col_im] - exit_ref[f, 1, at, col]
                wide_ref[at_f, col] = d_re
                wide_ref[at_f, col_im] = d_im
                p_re = probe_ref[f, 0, at, col]
                p_im = probe_ref[f, 1, at, col]
                parts[0].append(pltpu.roll(p_re * d_re + p_im * d_im, shift, 1))
                parts[1].append(pltpu.roll(p_re * d_im - p_im * d_re, shift, 1))
                parts[2].append(pltpu.roll(p_re * p_re + p_im * p_im, shift, 1))
            for q in range(3):
                for t in range(lanes + 1):
                    before = parts[q][t - 1] if t > 0 else 0.0
                    after = parts[q][t] if t < lanes else 0.0
                    value = jnp.where(column < shift, before, after)
                    tot_ref[q, tile + t, rows, :] = tot_ref[q, tile + t, rows, :] + value
        return carry

    lax.fori_loop(0, n // ROWS, place, 0)
    stores = []
    for i, (dst, a, b) in enumerate(
        ((t_corner_ref, n, lanes), (t_right_ref, 0, lanes), (t_below_ref, n, 0), (t_own_ref, 0, 0))
    ):
        for lane in range(lanes):
            stores.append(
                pltpu.make_async_copy(
                    quarter(tot_ref, a, b, lane), strip(dst, lane), out_sem.at[i * lanes + lane]
                )
            )
    for store in stores:
        store.start()

    def finish(b, carry):
        at = pl.ds(pl.multiple_of(b * 16, 16), 16)
        for lane in range(lanes):
            col = slice(lane * 128, lane * 128 + 128)
            col_im = slice(n + lane * 128, n + lane * 128 + 128)
            slopes = []
            for f in range(frames):
                at_f = pl.ds(pl.multiple_of(f * n + b * 16, 16), 16)
                d_re = wide_ref[at_f, col]
                d_im = wide_ref[at_f, col_im]
                o_re = grads_ref[f, 0, at, col]
                o_im = grads_ref[f, 1, at, col]
                g_re = o_re * d_re + o_im * d_im
                g_im = o_re * d_im - o_im * d_re
                grads_ref[f, 0, at, col] = g_re
                grads_ref[f, 1, at, col] = g_im
                slopes.append((jnp.where(is_first, g_re, g_im), jnp.where(is_first, g_im, g_re)))
            for k in range(modes):
                keep = weights[0][k] * slopes[0][0]
                give = weights[0][k] * slopes[0][1]
                for f in range(1, frames):
                    keep = keep + weights[f][k] * slopes[f][0]
                    give = give + weights[f][k] * slopes[f][1]
                for i in range(2):
                    tile = (2 * b + i) * lanes + lane
                    keep_ref[tile, k] = keep[8 * i : 8 * i + 8]
                    give_ref[tile, k] = give[8 * i : 8 * i + 8]
        return carry

    for half in range(2):
        lax.fori_loop(half * (n // 32), (half + 1) * (n // 32), finish, 0)
        at = pl.ds(half * (n // 2), n // 2)
        store = pltpu.make_async_copy(
            grads_ref.at[:, :, at, :], grads_hbm.at[:, :, at, :], side_sem.at[2 + half]
        )
        store.start()
        stores.append(store)
    for store in stores:
        store.wait()


def run_frames(core, positions, count, coefficients, blocks, amplitudes, modes, tables, staged):
    frames, n = amplitudes.shape[0], amplitudes.shape[1]
    k = modes.shape[0]
    tiles = n * n // 1024
    smem = pl.BlockSpec(memory_space=pltpu.SMEM)
    vmem = pl.BlockSpec(memory_space=pltpu.VMEM)
    hbm = pl.BlockSpec(memory_space=pl.ANY)
    piece = pltpu.VMEM((tiles, k, 8, 128), F32)
    quarter = pltpu.HBM((3, n, n), F32)
    return pl.pallas_call(
        functools.partial(frames_kernel, staged=staged),
        out_shape=(piece, piece, pltpu.HBM((frames, 2, n, n), F32)) + (quarter,) * 4,
        in_specs=[smem] * 4 + [hbm] + [vmem] * 3 + [hbm, hbm if staged else vmem] + [vmem] * 2,
        out_specs=(vmem,) * 2 + (hbm,) * 5,
        compiler_params=SMALL,
        scratch_shapes=[
            pltpu.VMEM((2, 2 * n // 128, 2 * n, 128), F32),
            pltpu.VMEM((3, 2 * n // 128, 2 * n, 128), F32),
            pltpu.VMEM((frames, 2, n, n), F32),
            pltpu.VMEM((frames, 2, n, n), F32),
            pltpu.VMEM((2 * n, 2 * n), BF16),
            pltpu.VMEM((2 * n, 2 * n), BF16),
            pltpu.VMEM((2 * n, frames * n), BF16),
            pltpu.VMEM((frames * n, 2 * n), BF16),
            pltpu.VMEM((frames * n, 2 * n), F32),
            pltpu.VMEM((frames, n, n), BF16),
            pltpu.VMEM((frames, 2, n, n), F32),
            pltpu.VMEM(modes.shape if staged else (8, 128), F32),
            pltpu.SemaphoreType.DMA((4 * n // 128,)),
            pltpu.SemaphoreType.DMA((4 * n // 128,)),
            pltpu.SemaphoreType.DMA((4,)),
        ],
        name="frames",
    )(
        core, far(positions), count, far(coefficients) if staged else coefficients,
        far(blocks[0]) if staged else blocks[0], *map(near, blocks[1:]),
        far(amplitudes), far(modes) if staged else near(modes), *tables,
    )


def spread_kernel(got_ref, out_ref):
    total = jnp.sum(got_ref[...], axis=0)
    out_ref[...] = jnp.broadcast_to(total[None], out_ref.shape)


def run_spread(got):
    vmem = pl.BlockSpec(memory_space=pltpu.VMEM)
    return pl.pallas_call(
        spread_kernel,
        out_shape=pltpu.VMEM(got.shape, F32),
        in_specs=[vmem],
        out_specs=vmem,
        compiler_params=SMALL,
        name="spread",
    )(got)


def total_of(acc):
    across = jnp.sum(jnp.sum(acc, axis=0, keepdims=True), axis=1, keepdims=True)
    return jnp.broadcast_to(across, acc.shape)


def modes_kernel(
    core_ref, cnt_ref, coef_ref, mine_hbm, other_ref, old_hbm, grads_hbm, new_ref, out_coef_ref,
    raised_ref, old_ref, grads_ref, mine_ref, sem, *, root_total,
):
    part = old_ref.shape[2] // CHUNKS
    tiles = mine_ref.shape[0] // CHUNKS
    loads = []
    for i in range(CHUNKS):
        at = pl.ds(i * part, part)
        loads.append(pltpu.make_async_copy(old_hbm.at[:, :, at, :], old_ref.at[:, :, at, :], sem.at[i]))
        at = pl.ds(i * tiles, tiles)
        loads.append(pltpu.make_async_copy(mine_hbm.at[at], mine_ref.at[at], sem.at[CHUNKS + 1 + i]))
    grads_load = pltpu.make_async_copy(grads_hbm, grads_ref, sem.at[CHUNKS])
    for load in loads + [grads_load]:
        load.start()
    modes, n = old_ref.shape[0], old_ref.shape[2]
    frames = grads_ref.shape[0]
    pixels = n * n
    is_first = core_ref[0] == 0
    lanes = n // 128
    pairs = [(i, j) for j in range(modes) for i in range(j)]
    zero = jnp.zeros((8, 128), F32)

    def lift(t, acc):
        acc = list(acc)
        at = pl.ds(pl.multiple_of(t * 8, 8), 8)
        for lane in range(lanes):
            col = slice(lane * 128, lane * 128 + 128)
            tile = t * lanes + lane
            re, im = [], []
            for k in range(modes):
                mine = mine_ref[tile, k]
                other = other_ref[tile, k]
                s_re = jnp.where(is_first, mine, other)
                s_im = jnp.where(is_first, other, mine)
                re.append(old_ref[k, 0, at, col] + s_re * (1.0 / root_total))
                im.append(old_ref[k, 1, at, col] + s_im * (1.0 / root_total))
                raised_ref[k, 0, at, col] = re[k]
                raised_ref[k, 1, at, col] = im[k]
            for k in range(modes):
                acc[k] = acc[k] + (re[k] * re[k] + im[k] * im[k])
            for p, (i, j) in enumerate(pairs):
                acc[modes + 2 * p] = acc[modes + 2 * p] + (re[i] * re[j] + im[i] * im[j])
                acc[modes + 2 * p + 1] = acc[modes + 2 * p + 1] + (re[i] * im[j] - im[i] * re[j])
        return tuple(acc)

    acc = (zero,) * (modes + 2 * len(pairs))
    for i in range(CHUNKS):
        loads[2 * i].wait()
        loads[2 * i + 1].wait()
        acc = lax.fori_loop(i * (part // 8), (i + 1) * (part // 8), lift, acc)
    grads_load.wait()
    gram = [total_of(a) * (1.0 / pixels) for a in acc]
    upper = {}
    inverse = []
    for j in range(modes):
        for i in range(j):
            p = pairs.index((i, j))
            s_re = gram[modes + 2 * p]
            s_im = gram[modes + 2 * p + 1]
            for k in range(i):
                a_re, a_im = upper[k, i]
                b_re, b_im = upper[k, j]
                s_re = s_re - (a_re * b_re + a_im * b_im)
                s_im = s_im - (a_re * b_im - a_im * b_re)
            upper[i, j] = (s_re * inverse[i], s_im * inverse[i])
        diagonal = gram[j]
        for k in range(j):
            a_re, a_im = upper[k, j]
            diagonal = diagonal - (a_re * a_re + a_im * a_im)
        inverse.append(1.0 / jnp.sqrt(diagonal))

    def solve(t, acc):
        acc = list(acc)
        at = pl.ds(pl.multiple_of(t * 8, 8), 8)
        for lane in range(lanes):
            col = slice(lane * 128, lane * 128 + 128)
            basis = []
            for j in range(modes):
                v_re = raised_ref[j, 0, at, col]
                v_im = raised_ref[j, 1, at, col]
                for i in range(j):
                    r_re, r_im = upper[i, j]
                    q_re, q_im = basis[i]
                    v_re = v_re - (r_re * q_re - r_im * q_im)
                    v_im = v_im - (r_re * q_im + r_im * q_re)
                basis.append((v_re * inverse[j], v_im * inverse[j]))
                new_ref[j, 0, at, col] = basis[j][0]
                new_ref[j, 1, at, col] = basis[j][1]
            for j in range(modes):
                o_re = old_ref[j, 0, at, col]
                o_im = old_ref[j, 1, at, col]
                for k in range(modes):
                    s = j * modes + k
                    acc[s] = acc[s] + (basis[k][0] * o_re + basis[k][1] * o_im)
            for f in range(frames):
                g_re = grads_ref[f, 0, at, col]
                g_im = grads_ref[f, 1, at, col]
                for k in range(modes):
                    s = (modes + f) * modes + k
                    acc[s] = acc[s] + (basis[k][0] * g_re + basis[k][1] * g_im)
        return tuple(acc)

    acc = lax.fori_loop(0, n // 8, solve, (zero,) * ((modes + frames) * modes))
    dots = [jnp.sum(a) * (1.0 / pixels) for a in acc]
    for f in range(frames):
        for k in range(modes):
            value = 0.5 * dots[(modes + f) * modes + k]
            for j in range(modes):
                value = value + coef_ref[f, j] * dots[j * modes + k]
            out_coef_ref[f, k] = jnp.where(f < cnt_ref[0], value, coef_ref[f, k])


def run_modes(core, count, coefficients, mine, other, old, grads, root_total):
    smem = pl.BlockSpec(memory_space=pltpu.SMEM)
    vmem = pl.BlockSpec(memory_space=pltpu.VMEM)
    hbm = pl.BlockSpec(memory_space=pl.ANY)
    return pl.pallas_call(
        functools.partial(modes_kernel, root_total=root_total),
        out_shape=(
            jax.ShapeDtypeStruct(old.shape, F32),
            jax.ShapeDtypeStruct(coefficients.shape, F32),
        ),
        in_specs=[smem] * 3 + [hbm, vmem] + [hbm] * 2,
        out_specs=(vmem, smem),
        scratch_shapes=[
            pltpu.VMEM(old.shape, F32),
            pltpu.VMEM(old.shape, F32),
            pltpu.VMEM(grads.shape, F32),
            pltpu.VMEM(mine.shape, F32),
            pltpu.SemaphoreType.DMA((2 * CHUNKS + 1,)),
        ],
        compiler_params=SMALL,
        name="modes",
    )(core, count, coefficients, far(mine), near(other), far(old), far(grads))


def moves(scans, cols, down, over):
    pairs = []
    for s in range(scans):
        for c in range(cols):
            if 0 <= s + down < scans and 0 <= c + over < cols:
                pairs.append((s * cols + c, (s + down) * cols + c + over))
    return pairs


def on_device(object_field, amplitudes, positions, frame_count, coefficients, probe_modes):
    frames, length = amplitudes.shape[0], amplitudes.shape[1]
    cols = lax.axis_size("y")
    scans = lax.axis_size(SCAN)
    root_total = math.sqrt(frames * scans * cols)
    core = lax.axis_index("core").astype(jnp.int32).reshape(1)
    swap = [(0, 1), (1, 0)]

    def widen(block):
        right = lax.ppermute(block, ALL, moves(scans, cols, 0, -1))
        below = lax.ppermute(block, ALL, moves(scans, cols, -1, 0))
        corner = lax.ppermute(right, ALL, moves(scans, cols, -1, 0))
        return [block, right, below, corner]

    tables = lax.optimization_barrier(make_tables(length))
    blocks = widen(object_field)
    for iteration in range(ITERS):
        keep, give, grads, t_own, t_right, t_below, t_corner = run_frames(
            core, positions, frame_count, coefficients, blocks, amplitudes, probe_modes, tables,
            iteration == 0,
        )
        crossed = lax.ppermute(t_corner, ALL, moves(scans, cols, 1, 0))
        joined = t_right + crossed
        kept = keep + lax.ppermute(give, "core", swap)
        arrived = lax.ppermute(joined, ALL, moves(scans, cols, 0, 1))
        lowered = lax.ppermute(t_below, ALL, moves(scans, cols, 1, 0))
        got = lax.all_to_all(kept, CHIPS, split_axis=0, concat_axis=0, tiled=True)
        settled = t_own + arrived + lowered
        object_field = object_field + settled[:2] / (settled[2] + 1.0)
        if iteration + 1 < ITERS:
            blocks = widen(object_field)
        spread = run_spread(near(got))
        mine = lax.all_to_all(spread, CHIPS, split_axis=0, concat_axis=0, tiled=True)
        other = lax.ppermute(mine, "core", swap)
        probe_modes, coefficients = run_modes(
            core, frame_count, coefficients, mine, other, probe_modes, grads, root_total
        )
    return (object_field, probe_modes, coefficients)


def solution(mesh):
    scans, cols = mesh.shape["scan"], mesh.shape["col"]
    fine = Mesh(np.asarray(mesh.devices).reshape(4, scans // 8, 2, cols), ALL)
    placed = (
        P(None, SCAN, "y"),
        P(ALL, None, None),
        P(ALL, None),
        P(ALL),
        P(ALL, None),
        P(),
    )
    return jax.shard_map(
        on_device,
        mesh=fine,
        in_specs=placed,
        out_specs=(P(None, SCAN, "y"), P(), P(ALL, None)),
        check_vma=False,
    )
```
